32 devices in a mesh: band: 8 (over z, x), coef: 4 (over y, core).
Axes of the slice: x: 2, y: 2, z: 4, core: 2. Of those that a mesh axis runs over, the one named last changes fastest.
Arguments:
- coeffs: float32 [1024, 262144], P('band', 'coef'), may hold values from -320 to 320
- ref_block: float32 [1024, 262144], P('band', 'coef'), may hold values from -0.01171875 to 0.01171875
- index_map: int32 [262144], P('coef'), may hold values from 0 to 65535, as said below
- band_group: int32 [1024], P('band'), may hold values from 0 to 15
Outputs:
- ortho: float32 [1024, 262144], P('band', 'coef')
- band_residual: float32 [1024], P('band')
- group_residual: float32 [16], replicated
The draws below stay inside these ranges and needn't reach their ends.
Inputs may be any that keep to these rules, and one draw needn't show every extreme that they name: Within each aligned slab of 65536 coefficients, index_map holds every number of 0 to 65535 once.
All inputs are finite; a program needn't handle non-finite values.
Results may differ from the reference program's by a relative error of at most 0.000098.
Values sent between devices are 32-bit elements; how exact they have to be, the bound alone decides.
A program may use at most 384 MiB of HBM per device.

```python
import math
import jax
import jax.numpy as jnp
from jax import lax

NB = 1024
NG = 262144
NGROUPS = 16
GS = 65536


def shared_basis(key):
    base = jax.random.fold_in(key, 11)
    basis = jnp.clip(jax.random.normal(base, (NB, NG), jnp.float32), -6.0, 6.0)
    return basis


def slab_order(key):
    base = jax.random.fold_in(key, 23)
    slabs = NG // GS
    starts = jnp.arange(slabs)
    keys = jax.vmap(lambda number: jax.random.fold_in(base, number))(starts)
    return jax.vmap(lambda single: jax.random.permutation(single, GS))(keys).astype(jnp.int32)


def draw_coeffs(key, part):
    basis = shared_basis(key)
    mixing = jax.random.uniform(jax.random.fold_in(key, 31), (NB,), jnp.float32, 0.3, 0.6)
    scales = jnp.exp(jax.random.uniform(jax.random.fold_in(key, 37), (NB,), jnp.float32, 0.0, math.log(10.0)))
    mixed = basis + mixing[:, None] * jnp.roll(basis, 1, axis=0)
    return (scales[:, None] * mixed).astype(jnp.float32)


def draw_ref_block(key, part):
    basis = shared_basis(key)
    order = slab_order(key)
    slabs = NG // GS
    shaped = basis.reshape(NB, slabs, GS)
    moved = jnp.take_along_axis(shaped, order[None, :, :], axis=2).reshape(NB, NG)
    return (moved / math.sqrt(NG)).astype(jnp.float32)


def draw_index_map(key, part):
    return slab_order(key).reshape(NG).astype(jnp.int32)


def touch_ends(values, own_key, least, top_value):
    longest = values.shape.index(max(values.shape))
    spots = []
    for shift in (0, 1):
        where = [jax.random.randint(jax.random.fold_in(own_key, axis), (), 0, length) for axis, length in enumerate(values.shape)]
        where[longest] = (where[longest] + shift) % values.shape[longest]
        spots.append(tuple(where))
    return values.at[spots[0]].set(least).at[spots[1]].set(top_value)


def setup_inputs(seed: int = 0) -> dict:
    streams_of = jax.random.split(jax.random.key(seed), 5)
    coeffs = draw_coeffs(jax.random.fold_in(streams_of[4], 71), 0)
    ref_block = draw_ref_block(jax.random.fold_in(streams_of[4], 71), 0)
    index_map = draw_index_map(jax.random.fold_in(streams_of[4], 71), 0)
    band_group = touch_ends(jax.random.randint(streams_of[3], (NB,), 0, NGROUPS), jax.random.fold_in(streams_of[3], 1), 0, NGROUPS - 1).astype(jnp.int32)
    return dict(coeffs=coeffs, ref_block=ref_block, index_map=index_map, band_group=band_group)


def reference(coeffs, ref_block, index_map, band_group):
    margin = jnp.dot(coeffs.astype(jnp.float32), coeffs.T.astype(jnp.float32), precision=lax.Precision.HIGHEST, preferred_element_type=jnp.float32)
    factor = jnp.linalg.cholesky(margin)
    ortho = lax.linalg.triangular_solve(factor, coeffs, left_side=True, lower=True)
    slabs = NG // GS
    shaped = ortho.reshape(NB, slabs, GS)
    order = index_map.reshape(slabs, GS).astype(jnp.int32)
    aligned = jnp.take_along_axis(shaped, order[None, :, :], axis=2).reshape(NB, NG)
    squares = lax.optimization_barrier(jnp.sum((aligned - ref_block) ** 2, axis=1))
    band_residual = jnp.sqrt(squares + 1e-06)
    group_residual = jax.ops.segment_sum(band_residual, band_group, num_segments=NGROUPS) * (NGROUPS / NB)
    return (ortho, band_residual, group_residual.astype(jnp.float32))
```

```python
import jax
import jax.numpy as jnp
from jax import lax
from jax.sharding import PartitionSpec as P

NGROUPS = 16
BLOCK = 128
ROWS = 256


def high(a, b):
    return jnp.dot(a, b, precision=lax.Precision.HIGH, preferred_element_type=jnp.float32)


def highest(a, b):
    return jnp.dot(a, b, precision=lax.Precision.HIGHEST, preferred_element_type=jnp.float32)


def inverse_factor(margin):
    size = margin.shape[0]
    eye = jnp.eye(BLOCK, dtype=jnp.float32)
    rest = margin
    below = jnp.zeros((size, 0), jnp.float32)
    rows = []
    for start in range(0, size, BLOCK):
        corner = lax.linalg.cholesky(rest[:BLOCK, :BLOCK], symmetrize_input=False)
        inv = lax.linalg.triangular_solve(corner, eye, left_side=True, lower=True)
        row = jnp.concatenate([highest(inv, below[:BLOCK]), inv], axis=1) if start else inv
        rows.append(jnp.pad(row, ((0, 0), (0, size - row.shape[1]))))
        if start + BLOCK < size:
            panel = highest(rest[BLOCK:, :BLOCK], inv.T)
            change = highest(panel, row)
            below = jnp.pad(below[BLOCK:], ((0, 0), (0, BLOCK))) - change
            rest = rest[BLOCK:, BLOCK:] - highest(panel, panel.T)
    return jnp.concatenate(rows, axis=0)


def local(coeffs, ref_block, index_map, band_group):
    devices = lax.axis_size("band")
    bands, slab = coeffs.shape
    part = slab // devices
    total = bands * devices

    pieces = coeffs.reshape(bands, devices, part).transpose(1, 0, 2)
    columns = lax.all_to_all(pieces, "band", split_axis=0, concat_axis=0, tiled=True)
    columns = columns.reshape(total, part)

    _, inverse = lax.sort((index_map, jnp.arange(slab, dtype=jnp.int32)), num_keys=1)
    ref_own = jnp.take(ref_block, inverse, axis=1, unique_indices=True, mode="clip")

    tops = range(0, total, ROWS)
    strips = [high(columns[t : t + ROWS], columns[: t + ROWS].T) for t in tops]
    strips = lax.psum(jnp.concatenate(strips, axis=1), ("band", "coef"))
    lower, at = [], 0
    for t in tops:
        width = t + ROWS
        lower.append(jnp.pad(strips[:, at : at + width], ((0, 0), (0, total - width))))
        at += width
    lower = jnp.concatenate(lower, axis=0)
    low = jnp.tril(lower)
    margin = low + jnp.tril(lower, -1).T
    inv = inverse_factor(margin)

    ortho_cols = jnp.concatenate(
        [high(inv[t : t + ROWS, : t + ROWS], columns[: t + ROWS]) for t in tops], axis=0
    )
    back = lax.all_to_all(
        ortho_cols.reshape(devices, bands, part), "band", split_axis=0, concat_axis=0, tiled=True
    )
    ortho = back.transpose(1, 0, 2).reshape(bands, slab)
    squares = jnp.sum((ortho - ref_own) ** 2, axis=1)
    band_residual = jnp.sqrt(lax.psum(squares, "coef") + 1e-06)
    onehot = (band_group[:, None] == jnp.arange(NGROUPS, dtype=jnp.int32)[None, :]).astype(jnp.float32)
    terms = highest(band_residual, onehot)
    group_residual = lax.psum(terms, "band") * (NGROUPS / total)
    return (ortho, band_residual, group_residual)


def solution(mesh):
    return jax.shard_map(
        local,
        mesh=mesh,
        in_specs=(P("band", "coef"), P("band", "coef"), P("coef"), P("band")),
        out_specs=(P("band", "coef"), P("band"), P()),
        check_vma=False,
    )
```
